512 devices in a mesh: row: 16 (over y, core), col: 32 (over x, z).
Axes of the slice: x: 4, y: 8, z: 8, core: 2. Of those that a mesh axis runs over, the one named last changes fastest.
Arguments:
- outcome_vectors: bfloat16 [16384, 1024], P('row', 'col'), may hold values from -6 to 6
- u_factor: bfloat16 [32, 1024], P(None, 'col'), may hold values from -0.03125 to 0.03125
- v_factor: bfloat16 [32, 1024], P(None, 'col'), may hold values from -0.03125 to 0.03125
- outcome_index: int32 [16384], replicated, may hold values from 0 to 16383, each once
Outputs:
- factored: float32 [16384, 16384], P('row', 'col')
The draws below stay inside these ranges and needn't reach their ends.
All inputs are finite; a program needn't handle non-finite values.
Results may differ from the reference program's by a relative error of at most 0.0056.
Values may be sent and summed in bfloat16 or wider, within the bound.
A program may use at most 64 MiB of HBM per device.

```python
import jax
import jax.numpy as jnp
from jax import lax

N_EMB = 1024
R = 32
PANEL = 256
NPANEL = 2
M_ROWS = 16384


def block_levels(key, dims, pieces, smallest, largest):
    def one(position, shards_of):
        steps = jax.random.uniform(jax.random.fold_in(jax.random.fold_in(key, 6), position), (shards_of,), jnp.float32, smallest / len(pieces), largest / len(pieces))
        return jnp.repeat(jnp.exp(steps), dims[position] // shards_of).reshape((-1,) + (1,) * (len(dims) - position - 1))

    factor_of = one(*pieces[0])
    for cut in pieces[1:]:
        factor_of = factor_of * one(*cut)
    return factor_of


def centred(key, shape, width, reach, cuts=(), kind=jnp.bfloat16):
    loudness = block_levels(key, shape, cuts, -0.22, 0.18) if cuts else 1.0
    array = jax.random.normal(key, shape, jnp.float32) * width * loudness
    return jnp.minimum(jnp.maximum(array, -reach), reach).astype(kind)


def setup_inputs(seed: int = 0) -> dict:
    streams_of = jax.random.split(jax.random.key(seed), 5)
    outcome_vectors = centred(streams_of[0], (M_ROWS, N_EMB), 1.0, 6.0, ((0, 16), (1, 32)))
    u_factor = centred(streams_of[1], (R, N_EMB), (N_EMB * R) ** -0.5, 0.03125, ((1, 32),))
    v_factor = centred(streams_of[2], (R, N_EMB), (N_EMB * R) ** -0.5, 0.03125, ((1, 32),))
    outcome_index = jax.random.permutation(streams_of[3], M_ROWS).astype(jnp.int32)
    return dict(outcome_vectors=outcome_vectors, u_factor=u_factor, v_factor=v_factor, outcome_index=outcome_index)


def reference(outcome_vectors, u_factor, v_factor, outcome_index):
    factors = jnp.concatenate([u_factor, v_factor], axis=0)
    transformed = lax.dot_general(outcome_vectors.astype(jnp.float32), factors.astype(jnp.float32), (((1,), (1,)), ((), ())), preferred_element_type=jnp.float32).astype(jnp.bfloat16)
    picked = jnp.take(transformed, outcome_index.astype(jnp.int32), axis=0)
    first = picked[:, :R]
    second = picked[:, R:]
    gram_u = jnp.dot(first.astype(jnp.float32), first.T.astype(jnp.float32), preferred_element_type=jnp.float32)
    gram_v = jnp.dot(second.astype(jnp.float32), second.T.astype(jnp.float32), preferred_element_type=jnp.float32)
    schur = gram_u * gram_v + jnp.eye(M_ROWS, dtype=jnp.float32)
    for step in range(NPANEL):
        start = step * PANEL
        stop = start + PANEL
        lower = jnp.linalg.cholesky(schur[start:stop, start:stop])
        below = jax.scipy.linalg.solve_triangular(lower, schur[stop:, start:stop].T, lower=True).T
        update = jnp.dot(below, below.T, precision=lax.Precision.HIGHEST)
        schur = schur.at[stop:, stop:].add(-update)
        schur = schur.at[start:stop, start:stop].set(jnp.tril(lower))
        schur = schur.at[stop:, start:stop].set(below)
    return schur
```

```python
import functools

import jax
import jax.numpy as jnp
from jax import lax
from jax.experimental import pallas as pl
from jax.experimental.pallas import tpu as pltpu
from jax.sharding import PartitionSpec as P

F32 = jnp.float32
HI = lax.Precision.HIGHEST
NT = (((1,), (1,)), ((), ()))


def factor_block(load, store, lanes, subs):
    A = [load(t) for t in range(16)]
    for t in range(16):
        j0 = 8 * t
        C = {}
        for s in range(t, 16):
            for i in range(8):
                C[s, i] = jnp.broadcast_to(A[s][:, j0 + i : j0 + i + 1], (8, 128))
        for s in range(t + 1, 16):
            A[s] = jnp.where((lanes >= j0) & (lanes < j0 + 8), 0.0, A[s])
        R = A[t]
        piv = jnp.zeros((8, 128), F32)
        for i in range(8):
            p = jnp.broadcast_to(C[t, i][i : i + 1, :], (8, 128))
            ip = 1.0 / p
            piv = jnp.where(subs == i, p, piv)
            Ri = jnp.broadcast_to(R[i : i + 1, :], (8, 128))
            Ri = jnp.where(lanes == j0 + i, 1.0, Ri)
            rows = {l: jnp.broadcast_to(C[t, l][i : i + 1, :], (8, 128)) for l in range(i + 1, 8)}
            Rs = jnp.where((lanes > j0 + i) & (lanes < j0 + 8), 0.0, Ri)
            m = jnp.where(subs > i, C[t, i] * ip, 0.0)
            R = jnp.where((subs > i) & (lanes == j0 + i), 0.0, R) - m * Ri
            for l in range(i + 1, 8):
                C[t, l] = C[t, l] - m * rows[l]
            for s in range(t + 1, 16):
                m = C[s, i] * ip
                A[s] = A[s] - m * Rs
                for l in range(i + 1, 8):
                    C[s, l] = C[s, l] - m * rows[l]
        rs = lax.rsqrt(piv)
        inv = jnp.where(lanes < j0 + subs, R * rs, jnp.where(lanes == j0 + subs, rs, 0.0))
        store(t, inv)


def kernel(rc, idx_ref, tab_ref, out_ref, t2, g32, gu, gv, sx, inv_ref):
    r, c = rc() if callable(rc) else rc
    lanes = lax.broadcasted_iota(jnp.int32, (8, 128), 1)
    subs = lax.broadcasted_iota(jnp.int32, (8, 128), 0)

    def unpack(b, _):
        src = pl.multiple_of(b * 512, 512)
        for q in range(16):
            v = tab_ref[pl.ds(src + q * 32, 32), :].astype(F32)
            dst = pl.multiple_of(b * 1024, 1024)
            t2[pl.ds(dst + q * 32, 32), :] = v
            t2[pl.ds(dst + 512 + q * 32, 32), :] = pltpu.roll(v, 64, 1)
        return 0

    lax.fori_loop(0, 16, unpack, 0)

    def pick(n, base, dst):
        def body(i, _):
            for q in range(16):
                j = i * 16 + q
                g32[pl.ds(dst + j, 1), :] = t2[pl.ds(idx_ref[base + j], 1), :]
            return 0
        lax.fori_loop(0, n // 16, body, 0)

    pick(512, 0, 0)
    pick(512, c * 512, 512)
    pick(1024, r * 1024, 1024)
    wide = lax.broadcasted_iota(jnp.int32, (256, 128), 1)

    def masks(i, _):
        rows = pl.ds(pl.multiple_of(i * 256, 256), 256)
        g = g32[rows, :]
        gu[rows, :] = jnp.where(wide < 32, g, 0.0).astype(jnp.bfloat16)
        gv[rows, :] = jnp.where((wide >= 32) & (wide < 64), g, 0.0).astype(jnp.bfloat16)
        return 0

    lax.fori_loop(0, 8, masks, 0)

    def gram(rows, cols):
        a = lax.dot_general(gu[rows, :], gu[cols, :], NT, preferred_element_type=F32)
        b = lax.dot_general(gv[rows, :], gv[cols, :], NT, preferred_element_type=F32)
        return a * b

    il = lax.broadcasted_iota(jnp.int32, (256, 512), 0)
    ic = lax.broadcasted_iota(jnp.int32, (256, 512), 1)
    for i in range(8):
        rows = pl.ds(i * 256, 256)
        first = i * 256 if i < 2 else (c * 512 + (i - 2) * 256 if i < 4 else r * 1024 + (i - 4) * 256)
        sx[rows, :] = gram(rows, pl.ds(0, 512)) + jnp.where(il + first == ic, 1.0, 0.0)

    for k in range(4):
        cols = pl.ds(k * 128, 128)
        factor_block(
            lambda t: sx[pl.ds(k * 128 + 8 * t, 8), cols],
            lambda t, v: inv_ref.__setitem__((pl.ds(8 * t, 8), slice(None)), v),
            lanes, subs,
        )
        for i in range(8):
            rows = pl.ds(i * 256, 256)
            if i * 256 + 256 <= k * 128:
                continue
            sx[rows, cols] = lax.dot_general(sx[rows, cols], inv_ref[...], NT, precision=HI, preferred_element_type=F32)
        if k < 3:
            rest = pl.ds(k * 128 + 128, 384 - k * 128)
            for i in range(8):
                if i * 256 + 256 <= k * 128 + 128:
                    continue
                rows = pl.ds(i * 256, 256)
                sx[rows, rest] = sx[rows, rest] - lax.dot_general(
                    sx[rows, cols], sx[rest, cols], NT, precision=HI, preferred_element_type=F32)

    for i in range(4):
        rows = pl.ds(1024 + i * 256, 256)
        dst = pl.ds(i * 256, 256)
        grow = il + (r * 1024 + i * 256)
        s = gram(rows, pl.ds(512, 512)) + jnp.where(grow == ic + c * 512, 1.0, 0.0)
        b = sx[rows, :]

        @pl.when(c == 0)
        def _():
            lead = jnp.where(ic <= grow, b, jnp.where((grow < 256) & (ic >= 256), s, 0.0))
            out_ref[dst, :] = jnp.where(grow < 512, lead, b)

        @pl.when(c != 0)
        def _():
            keep = (grow >= 512) | ((grow >= 256) & (ic < 256))
            bm = jnp.where(keep, b, 0.0)
            out_ref[dst, :] = s - lax.dot_general(bm, sx[pl.ds(512, 512), :], NT, precision=HI, preferred_element_type=F32)


def local_part(rc):
    def f(idx, tab):
        return pl.pallas_call(
            functools.partial(kernel, rc),
            out_shape=jax.ShapeDtypeStruct((1024, 512), F32),
            in_specs=[pl.BlockSpec(memory_space=pltpu.SMEM), pl.BlockSpec(memory_space=pltpu.VMEM)],
            out_specs=pl.BlockSpec(memory_space=pltpu.VMEM),
            scratch_shapes=[
                pltpu.VMEM((16384, 128), F32),
                pltpu.VMEM((2048, 128), F32),
                pltpu.VMEM((2048, 128), jnp.bfloat16),
                pltpu.VMEM((2048, 128), jnp.bfloat16),
                pltpu.VMEM((2048, 512), F32),
                pltpu.VMEM((128, 128), F32),
            ],
            compiler_params=pltpu.CompilerParams(vmem_limit_bytes=60 << 20),
        )(idx, tab)
    return f


MESH = pl.DeviceIdType.MESH
BF16 = jnp.bfloat16


def share_kernel(nx, nz, ny, x_ref, u_ref, v_ref, out_ref, part, rx, sumx, rz, tab,
                 rx_s, rx_r, rz_s, rz_r, az_s, az_r, ax_s, ax_r, yp_s, yp_r, ym_s, ym_r, pc_s, pc_r, out_sem):
    row, col = lax.axis_index("row"), lax.axis_index("col")
    y, core = row // 2, row % 2
    x, z = col // nz, col % nz
    twin = row + 1 - 2 * core

    def at_x(d):
        return (row, (x + d) % nx * nz + z)

    def at_z(d):
        return (row, x * nz + (z + d) % nz)

    def at_y(d):
        return ((y + d) % ny * 2 + core, col)

    barrier = pltpu.get_barrier_semaphore()
    peers = [at_x(d) for d in range(1, nx)] + [at_z(d) for d in range(1, nz)] + [at_y(1), at_y(ny - 1), (twin, col)]
    for peer in peers:
        pl.semaphore_signal(barrier, inc=1, device_id=peer, device_id_type=MESH)

    def copy(src, dst, send, recv, peer):
        return pltpu.make_async_remote_copy(
            src_ref=src, dst_ref=dst, send_sem=send, recv_sem=recv, device_id=peer, device_id_type=MESH)

    u, v = u_ref[...], v_ref[...]
    zero = jnp.zeros_like(u)
    half = x_ref.shape[0] // 2
    low = jnp.concatenate([u, v, zero, zero], axis=0)
    high = jnp.concatenate([zero, zero, u, v], axis=0)
    both = lax.dot_general(x_ref[:half, :], low, NT, preferred_element_type=F32)
    both = both + lax.dot_general(x_ref[half:, :], high, NT, preferred_element_type=F32)
    part[...] = both.reshape(part.shape)
    pl.semaphore_wait(barrier, len(peers))

    sent = []

    def go(c):
        c.start()
        sent.append(c)

    for d in range(1, nx):
        go(copy(part.at[(x + d) % nx], rx.at[d - 1], rx_s.at[d - 1], rx_r.at[d - 1], at_x(d)))
    total = part[x]
    for d in range(1, nx):
        copy(part.at[x], rx.at[d - 1], rx_s.at[d - 1], rx_r.at[d - 1], at_x(d)).wait_recv()
        total = total + rx[d - 1]
    sumx[...] = total
    for d in range(1, nz):
        go(copy(sumx.at[(z + d) % nz], rz.at[d - 1], rz_s.at[d - 1], rz_r.at[d - 1], at_z(d)))
    tile = sumx[z]
    for d in range(1, nz):
        copy(sumx.at[z], rz.at[d - 1], rz_s.at[d - 1], rz_r.at[d - 1], at_z(d)).wait_recv()
        tile = tile + rz[d - 1]
    tab[row, x, z] = tile.astype(BF16)

    for d in range(1, nz):
        mine = tab.at[row, x, z]
        go(copy(mine, mine, az_s.at[d - 1], az_r.at[d - 1], at_z(d)))
    for d in range(1, nz):
        theirs = tab.at[row, x, (z + nz - d) % nz]
        copy(theirs, theirs, az_s.at[d - 1], az_r.at[d - 1], at_z(d)).wait_recv()
    for d in range(1, nx):
        mine = tab.at[row, x]
        go(copy(mine, mine, ax_s.at[d - 1], ax_r.at[d - 1], at_x(d)))

    def piece(away, e):
        return tab.at[(y + ny - away) % ny * 2 + core, (x + nx - e) % nx]

    def arrived(k, e, away):
        ref = piece(away, e)
        go(copy(ref, ref, pc_s.at[k, e], pc_r.at[k, e], (twin, col)))

    up, down = ny // 2, ny - 1 - ny // 2

    def reach(e):
        return (up, down) if e % 2 == 0 else (down, up)

    for e in range(nx):
        if e:
            theirs = piece(0, e)
            copy(theirs, theirs, ax_s.at[e - 1], ax_r.at[e - 1], at_x(e)).wait_recv()
        ref = piece(0, e)
        go(copy(ref, ref, yp_s.at[0, e], yp_r.at[0, e], at_y(1)))
        go(copy(ref, ref, ym_s.at[0, e], ym_r.at[0, e], at_y(ny - 1)))
        arrived(0, e, 0)
    for s in range(1, up + 1):
        for e in range(nx):
            plus, minus = reach(e)
            if s <= plus:
                ref = piece(s, e)
                copy(ref, ref, yp_s.at[s - 1, e], yp_r.at[s - 1, e], at_y(1)).wait_recv()
                if s < plus:
                    go(copy(ref, ref, yp_s.at[s, e], yp_r.at[s, e], at_y(1)))
                arrived(s, e, s)
            if s <= minus:
                ref = piece(ny - s, e)
                copy(ref, ref, ym_s.at[s - 1, e], ym_r.at[s - 1, e], at_y(ny - 1)).wait_recv()
                if s < minus:
                    go(copy(ref, ref, ym_s.at[s, e], ym_r.at[s, e], at_y(ny - 1)))
                arrived(ny - s, e, ny - s)
    for k in range(ny):
        for e in range(nx):
            ref = tab.at[(y + ny - k) % ny * 2 + 1 - core, (x + nx - e) % nx]
            copy(ref, ref, pc_s.at[k, e], pc_r.at[k, e], (twin, col)).wait_recv()
    done = pltpu.make_async_copy(tab, out_ref, out_sem)
    done.start()
    for c in sent:
        c.wait_send()
    done.wait()


def share(nx, nz, ny, vectors, u, v):
    rows = vectors.shape[0] // 2
    block = rows // (nx * nz)
    dma = pltpu.SemaphoreType.DMA
    tab = (2 * ny, nx, nz, block, 128)
    vm = pl.BlockSpec(memory_space=pltpu.VMEM)
    pairs = []
    for shape in ((nx - 1,), (nz - 1,), (nz - 1,), (nx - 1,), (ny // 2, nx), (ny // 2, nx), (ny, nx)):
        pairs += [dma(shape), dma(shape)]
    return pl.pallas_call(
        functools.partial(share_kernel, nx, nz, ny),
        out_shape=jax.ShapeDtypeStruct(tab, BF16),
        in_specs=[vm] * 3,
        out_specs=pl.BlockSpec(memory_space=pl.ANY),
        scratch_shapes=[
            pltpu.VMEM((nx, nz, block, 128), F32),
            pltpu.VMEM((nx - 1, nz, block, 128), F32),
            pltpu.VMEM((nz, block, 128), F32),
            pltpu.VMEM((nz - 1, block, 128), F32),
            pltpu.VMEM(tab, BF16),
        ] + pairs + [dma],
        compiler_params=pltpu.CompilerParams(collective_id=0, has_side_effects=True, vmem_limit_bytes=32 << 20),
    )(vectors, u, v)


def body(outcome_vectors, u_factor, v_factor, outcome_index):
    table = share(4, 8, 8, outcome_vectors, u_factor, v_factor)
    return local_part(lambda: (lax.axis_index("row"), lax.axis_index("col")))(outcome_index, table.reshape(-1, 128))


def solution(mesh):
    placed = (P("row", "col"), P(None, "col"), P(None, "col"), P())
    return jax.shard_map(
        body, mesh=mesh, in_specs=placed, out_specs=P("row", "col"), check_vma=False
    )
```

```python
import functools

import jax
import jax.numpy as jnp
from jax import lax
from jax.experimental import pallas as pl
from jax.experimental.pallas import tpu as pltpu
from jax.sharding import PartitionSpec as P

F32 = jnp.float32
HI = lax.Precision.HIGHEST
NT = (((1,), (1,)), ((), ()))


def factor_block(load, store, lanes, subs):
    A = [load(t) for t in range(16)]
    for t in range(16):
        j0 = 8 * t
        C = {}
        for s in range(t, 16):
            for i in range(8):
                C[s, i] = jnp.broadcast_to(A[s][:, j0 + i : j0 + i + 1], (8, 128))
        for s in range(t + 1, 16):
            A[s] = jnp.where((lanes >= j0) & (lanes < j0 + 8), 0.0, A[s])
        R = A[t]
        piv = jnp.zeros((8, 128), F32)
        for i in range(8):
            p = jnp.broadcast_to(C[t, i][i : i + 1, :], (8, 128))
            ip = 1.0 / p
            piv = jnp.where(subs == i, p, piv)
            Ri = jnp.broadcast_to(R[i : i + 1, :], (8, 128))
            Ri = jnp.where(lanes == j0 + i, 1.0, Ri)
            rows = {l: jnp.broadcast_to(C[t, l][i : i + 1, :], (8, 128)) for l in range(i + 1, 8)}
            Rs = jnp.where((lanes > j0 + i) & (lanes < j0 + 8), 0.0, Ri)
            m = jnp.where(subs > i, C[t, i] * ip, 0.0)
            R = jnp.where((subs > i) & (lanes == j0 + i), 0.0, R) - m * Ri
            for l in range(i + 1, 8):
                C[t, l] = C[t, l] - m * rows[l]
            for s in range(t + 1, 16):
                m = C[s, i] * ip
                A[s] = A[s] - m * Rs
                for l in range(i + 1, 8):
                    C[s, l] = C[s, l] - m * rows[l]
        rs = lax.rsqrt(piv)
        inv = jnp.where(lanes < j0 + subs, R * rs, jnp.where(lanes == j0 + subs, rs, 0.0))
        store(t, inv)


def split(x):
    high = x.astype(jnp.bfloat16)
    return high, (x - high.astype(F32)).astype(jnp.bfloat16)


def dot(a, b):
    return lax.dot_general(a, b, NT, preferred_element_type=F32)


def kernel(rc, idx_ref, tab_ref, out_ref, t2, g32, gu, gv, sx, inv_ref, ch, cl):
    r, c = rc() if callable(rc) else rc
    lanes = lax.broadcasted_iota(jnp.int32, (8, 128), 1)
    subs = lax.broadcasted_iota(jnp.int32, (8, 128), 0)

    def unpack(b, _):
        for core in range(2):
            for x in range(4):
                for a in range(8):
                    y, z = (a, b) if core == 0 else (b, a)
                    tile = tab_ref[core, b, x, a].astype(F32)
                    dst = pl.multiple_of((y * 2 + core) * 1024 + (x * 8 + z) * 16, 16)
                    t2[pl.ds(dst, 16), :] = tile
                    t2[pl.ds(dst + 512, 16), :] = pltpu.roll(tile, 64, 1)
        return 0

    lax.fori_loop(0, 8, unpack, 0)

    def pick(n, base, dst):
        def body(i, _):
            for q in range(16):
                j = i * 16 + q
                g32[pl.ds(dst + j, 1), :] = t2[pl.ds(idx_ref[base + j], 1), :]
            return 0
        lax.fori_loop(0, n // 16, body, 0)

    pick(512, 0, 0)
    pick(512, c * 512, 512)
    pick(1024, r * 1024, 1024)
    wide = lax.broadcasted_iota(jnp.int32, (256, 128), 1)

    def masks(i, _):
        rows = pl.ds(pl.multiple_of(i * 256, 256), 256)
        g = g32[rows, :]
        gu[rows, :] = jnp.where(wide < 32, g, 0.0).astype(jnp.bfloat16)
        gv[rows, :] = jnp.where((wide >= 32) & (wide < 64), g, 0.0).astype(jnp.bfloat16)
        return 0

    lax.fori_loop(0, 8, masks, 0)

    def gram(rows, cols):
        a = lax.dot_general(gu[rows, :], gu[cols, :], NT, preferred_element_type=F32)
        b = lax.dot_general(gv[rows, :], gv[cols, :], NT, preferred_element_type=F32)
        return a * b

    il = lax.broadcasted_iota(jnp.int32, (256, 512), 0)
    ic = lax.broadcasted_iota(jnp.int32, (256, 512), 1)
    for i in range(8):
        rows = pl.ds(i * 256, 256)
        first = i * 256 if i < 2 else (c * 512 + (i - 2) * 256 if i < 4 else r * 1024 + (i - 4) * 256)
        sx[rows, :] = gram(rows, pl.ds(0, 512)) + jnp.where(il + first == ic, 1.0, 0.0)

    for k in range(4):
        cols = pl.ds(k * 128, 128)
        factor_block(
            lambda t: sx[pl.ds(k * 128 + 8 * t, 8), cols],
            lambda t, v: inv_ref.__setitem__((pl.ds(8 * t, 8), slice(None)), v),
            lanes, subs,
        )
        for i in range(8):
            rows = pl.ds(i * 256, 256)
            if i * 256 + 256 <= k * 128:
                continue
            sx[rows, cols] = lax.dot_general(sx[rows, cols], inv_ref[...], NT, precision=HI, preferred_element_type=F32)
        if k < 3:
            rest = pl.ds(k * 128 + 128, 384 - k * 128)
            for i in range(8):
                if i * 256 + 256 <= k * 128 + 128:
                    continue
                rows = pl.ds(i * 256, 256)
                sx[rows, rest] = sx[rows, rest] - lax.dot_general(
                    sx[rows, cols], sx[rest, cols], NT, precision=HI, preferred_element_type=F32)

    ch[...], cl[...] = split(sx[pl.ds(512, 512), :])
    for i in range(4):
        rows = pl.ds(1024 + i * 256, 256)
        dst = pl.ds(i * 256, 256)
        grow = il + (r * 1024 + i * 256)
        s = gram(rows, pl.ds(512, 512)) + jnp.where(grow == ic + c * 512, 1.0, 0.0)
        b = sx[rows, :]

        @pl.when(c == 0)
        def _():
            lead = jnp.where(ic <= grow, b, jnp.where((grow < 256) & (ic >= 256), s, 0.0))
            out_ref[dst, :] = jnp.where(grow < 512, lead, b)

        @pl.when(c != 0)
        def _():
            keep = (grow >= 512) | ((grow >= 256) & (ic < 256))
            bm = jnp.where(keep, b, 0.0)
            bh, bl = split(bm)
            out_ref[dst, :] = s - (dot(bh, ch[...]) + (dot(bh, cl[...]) + dot(bl, ch[...])))


def local_part(rc):
    def f(idx, tab):
        return pl.pallas_call(
            functools.partial(kernel, rc),
            out_shape=jax.ShapeDtypeStruct((1024, 512), F32),
            in_specs=[pl.BlockSpec(memory_space=pltpu.SMEM), pl.BlockSpec(memory_space=pltpu.VMEM)],
            out_specs=pl.BlockSpec(memory_space=pltpu.VMEM),
            scratch_shapes=[
                pltpu.VMEM((16384, 128), F32),
                pltpu.VMEM((2048, 128), F32),
                pltpu.VMEM((2048, 128), jnp.bfloat16),
                pltpu.VMEM((2048, 128), jnp.bfloat16),
                pltpu.VMEM((2048, 512), F32),
                pltpu.VMEM((128, 128), F32),
                pltpu.VMEM((512, 512), jnp.bfloat16),
                pltpu.VMEM((512, 512), jnp.bfloat16),
            ],
            compiler_params=pltpu.CompilerParams(vmem_limit_bytes=24 << 20),
        )(idx, tab)
    return f


MESH = pl.DeviceIdType.MESH
BF16 = jnp.bfloat16

def share_kernel(nx, n, x_ref, u_ref, v_ref, tab, xs, fs, sumx, rz, mine,
                 own_s, xs_s, xs_r, rz_s, rz_r, aa_s, aa_r, ax_s, ax_r, bp_s, bp_r, bm_s, bm_r, tw_s, tw_r):
    row, col = lax.axis_index("row"), lax.axis_index("col")
    y, core = row // 2, row % 2
    x, z = col // n, col % n
    other = 1 - core
    a, b = y * other + z * core, z * other + y * core
    twin = (row + 1 - 2 * core, col)

    def at_x(d):
        return (row, (x + d) % nx * n + z)

    def at_z(d):
        return (row, x * n + (z + d) % n)

    def at_y(d):
        return ((y + d) % n * 2 + core, col)

    def at_a(d):
        return (((y + d * other) % n) * 2 + core, x * n + (z + d * core) % n)

    def at_b(d):
        return (((y + d * core) % n) * 2 + core, x * n + (z + d * other) % n)

    barrier = pltpu.get_barrier_semaphore()
    peers = [at_x(d) for d in range(1, nx)] + [f(d) for f in (at_z, at_y) for d in range(1, n)] + [twin]
    for peer in peers:
        pl.semaphore_signal(barrier, inc=1, device_id=peer, device_id_type=MESH)

    def copy(src, dst, send, recv, peer):
        return pltpu.make_async_remote_copy(
            src_ref=src, dst_ref=dst, send_sem=send, recv_sem=recv, device_id=peer, device_id_type=MESH)

    half = x_ref.shape[1] // 2
    wide = half // nx

    def slices(to):
        lanes = pl.multiple_of(to * wide, wide)
        return [x_ref.at[:, pl.ds(lanes, wide)], x_ref.at[:, pl.ds(half + lanes, wide)], u_ref, v_ref]

    def slots(d):
        return [xs.at[d, 0], xs.at[d, 1], fs.at[d, 0], fs.at[d, 1]]

    own = [pltpu.make_async_copy(s, t, own_s.at[i]) for i, (s, t) in enumerate(zip(slices(x), slots(0)))]
    for c in own:
        c.start()
    pl.semaphore_wait(barrier, len(peers))

    sent = []

    def go(c):
        c.start()
        sent.append(c)

    def finish():
        for c in sent:
            c.wait_send()

    for d in range(1, nx):
        for i, (s, t) in enumerate(zip(slices((x + d) % nx), slots(d))):
            go(copy(s, t, xs_s.at[d - 1, i], xs_r.at[d - 1, i], at_x(d)))
    for c in own:
        c.wait()

    def product(d):
        f = fs[d].reshape(-1, fs.shape[-1])
        zero = jnp.zeros_like(f)
        over = (((0,), (1,)), ((), ()))
        return lax.dot_general(xs[d, 0], jnp.concatenate([f, zero], axis=0), over, preferred_element_type=F32) + \
            lax.dot_general(xs[d, 1], jnp.concatenate([zero, f], axis=0), over, preferred_element_type=F32)

    total = product(0)
    for d in range(1, nx):
        for i, (s, t) in enumerate(zip(slices(x), slots(d))):
            copy(s, t, xs_s.at[d - 1, i], xs_r.at[d - 1, i], at_x(d)).wait_recv()
        total = total + product(d)
    sumx[...] = total.reshape(sumx.shape)

    for d in range(1, n):
        go(copy(sumx.at[(z + d) % n], rz.at[d - 1], rz_s.at[d - 1], rz_r.at[d - 1], at_z(d)))
    tile = sumx[z]
    for d in range(1, n):
        copy(sumx.at[z], rz.at[d - 1], rz_s.at[d - 1], rz_r.at[d - 1], at_z(d)).wait_recv()
        tile = tile + rz[d - 1]
    mine[...] = tile.astype(BF16)

    keep = pltpu.make_async_copy(mine, tab.at[core, b, x, a], own_s.at[4])
    keep.start()
    for d in range(1, n):
        go(copy(mine, tab.at[core, b, x, a], aa_s.at[d - 1], aa_r.at[d - 1], at_a(d)))
    keep.wait()
    for d in range(1, n):
        copy(mine, tab.at[core, b, x, (a + n - d) % n], aa_s.at[d - 1], aa_r.at[d - 1], at_a(d)).wait_recv()

    def piece(away, e):
        return tab.at[core, (b + n - away) % n, (x + nx - e) % nx]

    for d in range(1, nx):
        go(copy(piece(0, 0), piece(0, 0), ax_s.at[d - 1], ax_r.at[d - 1], at_x(d)))

    def pass_on(k, e):
        go(copy(piece(k, e), piece(k, e), tw_s.at[k, e], tw_r.at[k, e], twin))

    def reach(e):
        return (n // 2, n - 1 - n // 2) if e % 2 == 0 else (n - 1 - n // 2, n // 2)

    for e in range(nx):
        if e:
            copy(piece(0, e), piece(0, e), ax_s.at[e - 1], ax_r.at[e - 1], at_x(e)).wait_recv()
        go(copy(piece(0, e), piece(0, e), bp_s.at[0, e], bp_r.at[0, e], at_b(1)))
        go(copy(piece(0, e), piece(0, e), bm_s.at[0, e], bm_r.at[0, e], at_b(n - 1)))
        pass_on(0, e)
    for s in range(1, n // 2 + 1):
        for e in range(nx):
            plus, minus = reach(e)
            for far, k, ss, rr, to in ((plus, s, bp_s, bp_r, 1), (minus, n - s, bm_s, bm_r, n - 1)):
                if s > far:
                    continue
                ref = piece(k, e)
                copy(ref, ref, ss.at[s - 1, e], rr.at[s - 1, e], at_b(to)).wait_recv()
                if s < far:
                    go(copy(ref, ref, ss.at[s, e], rr.at[s, e], at_b(to)))
                pass_on(k, e)
    theirs = z * core + y * other
    for k in range(n):
        for e in range(nx):
            ref = tab.at[other, (theirs + n - k) % n, (x + nx - e) % nx]
            copy(ref, ref, tw_s.at[k, e], tw_r.at[k, e], twin).wait_recv()
    finish()


def share(nx, n, vectors, u, v):
    depth, rows = vectors.shape
    block = rows // 2 // (nx * n)
    dma = pltpu.SemaphoreType.DMA
    tab = (2, n, nx, n, block, 128)
    hbm = pl.BlockSpec(memory_space=pltpu.MemorySpace.HBM)
    pairs = []
    for shape in ((nx - 1, 4), (n - 1,), (n - 1,), (nx - 1,), (n // 2, nx), (n // 2, nx), (n, nx)):
        pairs += [dma(shape), dma(shape)]
    return pl.pallas_call(
        functools.partial(share_kernel, nx, n),
        out_shape=jax.ShapeDtypeStruct(tab, BF16),
        in_specs=[hbm] * 3,
        out_specs=pl.BlockSpec(memory_space=pl.ANY),
        scratch_shapes=[
            pltpu.VMEM((nx, 2, depth, rows // 2 // nx), BF16),
            pltpu.VMEM((nx, 2) + u.shape, BF16),
            pltpu.VMEM((n, block, 128), F32),
            pltpu.VMEM((n - 1, block, 128), F32),
            pltpu.VMEM((block, 128), BF16),
            dma((5,)),
        ] + pairs,
        compiler_params=pltpu.CompilerParams(collective_id=0, has_side_effects=True, vmem_limit_bytes=8 << 20),
    )(vectors, u, v)


def in_hbm(t):
    return pltpu.with_memory_space_constraint(t, pltpu.MemorySpace.HBM)


def body(outcome_vectors, u_factor, v_factor, outcome_index):
    table = share(4, 8, in_hbm(outcome_vectors.T), in_hbm(u_factor), in_hbm(v_factor))
    return local_part(lambda: (lax.axis_index("row"), lax.axis_index("col")))(outcome_index, table)


def solution(mesh):
    placed = (P("row", "col"), P(None, "col"), P(None, "col"), P())
    return jax.shard_map(
        body, mesh=mesh, in_specs=placed, out_specs=P("row", "col"), check_vma=False
    )
```

```python
import functools

import jax
import jax.numpy as jnp
from jax import lax
from jax.experimental import pallas as pl
from jax.experimental.pallas import tpu as pltpu
from jax.sharding import PartitionSpec as P

F32 = jnp.float32
HI = lax.Precision.HIGHEST
NT = (((1,), (1,)), ((), ()))


def spread(x, j):
    return jnp.take_along_axis(x, jnp.full((8, 128), j, jnp.int32), axis=1)


def row_of(x, i):
    return jnp.broadcast_to(x[i : i + 1, :], (8, 128))


def factor_block(load, store, lanes, subs):
    A = [load(t) for t in range(16)]
    for t in range(16):
        j0 = 8 * t
        inside = (lanes >= j0) & (lanes < j0 + 8)
        C = [spread(A[t], j0 + i) for i in range(8)]
        R = A[t]
        piv = jnp.zeros((8, 128), F32)
        rows, outer = {}, []
        for i in range(8):
            p = row_of(C[i], i)
            ip = 1.0 / p
            piv = jnp.where(subs == i, p, piv)
            Ri = jnp.where(lanes == j0 + i, 1.0, row_of(R, i)) * ip
            for l in range(i + 1, 8):
                rows[i, l] = row_of(C[l], i) * ip
            m = jnp.where(subs > i, C[i], 0.0)
            R = jnp.where((subs > i) & (lanes == j0 + i), 0.0, R) - m * Ri
            for l in range(i + 1, 8):
                C[l] = C[l] - m * rows[i, l]
            outer.append(jnp.where((lanes > j0 + i) & (lanes < j0 + 8), 0.0, Ri))
        rs = lax.rsqrt(piv)
        store(t, jnp.where(lanes < j0 + subs, R * rs, jnp.where(lanes == j0 + subs, rs, 0.0)))
        for s in range(t + 1, 16):
            D = [spread(A[s], j0 + i) for i in range(8)]
            q = jnp.where(inside, 0.0, A[s])
            for i in range(8):
                q = q - D[i] * outer[i]
                for l in range(i + 1, 8):
                    D[l] = D[l] - D[i] * rows[i, l]
            A[s] = q


def split(x):
    high = x.astype(jnp.bfloat16)
    return high, (x - high.astype(F32)).astype(jnp.bfloat16)


def dot(a, b):
    return lax.dot_general(a, b, NT, preferred_element_type=F32)


def kernel(rc, idx_ref, tab_ref, out_ref, t2, g32, gu, gv, sx, inv_ref, ch, cl):
    r, c = rc() if callable(rc) else rc
    lanes = lax.broadcasted_iota(jnp.int32, (8, 128), 1)
    subs = lax.broadcasted_iota(jnp.int32, (8, 128), 0)

    def unpack(b, _):
        for core in range(2):
            for x in range(4):
                for a in range(8):
                    y, z = (a, b) if core == 0 else (b, a)
                    tile = tab_ref[core, b, x, a].astype(F32)
                    dst = pl.multiple_of((y * 2 + core) * 1024 + (x * 8 + z) * 16, 16)
                    t2[pl.ds(dst, 16), :] = tile
                    t2[pl.ds(dst + 512, 16), :] = pltpu.roll(tile, 64, 1)
        return 0

    lax.fori_loop(0, 8, unpack, 0)

    def pick(n, base, dst):
        def body(i, _):
            for q in range(16):
                j = i * 16 + q
                g32[pl.ds(dst + j, 1), :] = t2[pl.ds(idx_ref[base + j], 1), :]
            return 0
        lax.fori_loop(0, n // 16, body, 0)

    pick(512, 0, 0)
    pick(512, c * 512, 512)
    pick(1024, r * 1024, 1024)
    wide = lax.broadcasted_iota(jnp.int32, (256, 128), 1)

    def masks(i, _):
        rows = pl.ds(pl.multiple_of(i * 256, 256), 256)
        g = g32[rows, :]
        gu[rows, :] = jnp.where(wide < 32, g, 0.0).astype(jnp.bfloat16)
        gv[rows, :] = jnp.where((wide >= 32) & (wide < 64), g, 0.0).astype(jnp.bfloat16)
        return 0

    lax.fori_loop(0, 8, masks, 0)

    def gram(rows, cols):
        a = lax.dot_general(gu[rows, :], gu[cols, :], NT, preferred_element_type=F32)
        b = lax.dot_general(gv[rows, :], gv[cols, :], NT, preferred_element_type=F32)
        return a * b

    il = lax.broadcasted_iota(jnp.int32, (256, 512), 0)
    ic = lax.broadcasted_iota(jnp.int32, (256, 512), 1)
    for i in range(8):
        rows = pl.ds(i * 256, 256)
        first = i * 256 if i < 2 else (c * 512 + (i - 2) * 256 if i < 4 else r * 1024 + (i - 4) * 256)
        sx[rows, :] = gram(rows, pl.ds(0, 512)) + jnp.where(il + first == ic, 1.0, 0.0)

    for k in range(4):
        cols = pl.ds(k * 128, 128)
        factor_block(
            lambda t: sx[pl.ds(k * 128 + 8 * t, 8), cols],
            lambda t, v: inv_ref.__setitem__((pl.ds(8 * t, 8), slice(None)), v),
            lanes, subs,
        )
        for i in range(8):
            rows = pl.ds(i * 256, 256)
            if i * 256 + 256 <= k * 128:
                continue
            sx[rows, cols] = lax.dot_general(sx[rows, cols], inv_ref[...], NT, precision=HI, preferred_element_type=F32)
        if k < 3:
            rest = pl.ds(k * 128 + 128, 384 - k * 128)
            for i in range(8):
                if i * 256 + 256 <= k * 128 + 128:
                    continue
                rows = pl.ds(i * 256, 256)
                sx[rows, rest] = sx[rows, rest] - lax.dot_general(
                    sx[rows, cols], sx[rest, cols], NT, precision=HI, preferred_element_type=F32)

    ch[...], cl[...] = split(sx[pl.ds(512, 512), :])
    for i in range(4):
        rows = pl.ds(1024 + i * 256, 256)
        dst = pl.ds(i * 256, 256)
        grow = il + (r * 1024 + i * 256)
        s = gram(rows, pl.ds(512, 512)) + jnp.where(grow == ic + c * 512, 1.0, 0.0)
        b = sx[rows, :]

        @pl.when(c == 0)
        def _():
            lead = jnp.where(ic <= grow, b, jnp.where((grow < 256) & (ic >= 256), s, 0.0))
            out_ref[dst, :] = jnp.where(grow < 512, lead, b)

        @pl.when(c != 0)
        def _():
            keep = (grow >= 512) | ((grow >= 256) & (ic < 256))
            bm = jnp.where(keep, b, 0.0)
            bh, bl = split(bm)
            out_ref[dst, :] = s - (dot(bh, ch[...]) + (dot(bh, cl[...]) + dot(bl, ch[...])))


def local_part(rc):
    def f(idx, tab):
        return pl.pallas_call(
            functools.partial(kernel, rc),
            out_shape=jax.ShapeDtypeStruct((1024, 512), F32),
            in_specs=[pl.BlockSpec(memory_space=pltpu.SMEM), pl.BlockSpec(memory_space=pltpu.VMEM)],
            out_specs=pl.BlockSpec(memory_space=pltpu.VMEM),
            scratch_shapes=[
                pltpu.VMEM((16384, 128), F32),
                pltpu.VMEM((2048, 128), F32),
                pltpu.VMEM((2048, 128), jnp.bfloat16),
                pltpu.VMEM((2048, 128), jnp.bfloat16),
                pltpu.VMEM((2048, 512), F32),
                pltpu.VMEM((128, 128), F32),
                pltpu.VMEM((512, 512), jnp.bfloat16),
                pltpu.VMEM((512, 512), jnp.bfloat16),
            ],
            compiler_params=pltpu.CompilerParams(vmem_limit_bytes=24 << 20),
        )(idx, tab)
    return f


MESH = pl.DeviceIdType.MESH
BF16 = jnp.bfloat16

def share_kernel(nx, n, x_ref, u_ref, v_ref, tab, xs, fs, sumx, rz, mine,
                 own_s, xs_s, xs_r, rz_s, rz_r, aa_s, aa_r, ax_s, ax_r, bb_s, bb_r, tw_s, tw_r):
    row, col = lax.axis_index("row"), lax.axis_index("col")
    y, core = row // 2, row % 2
    x, z = col // n, col % n
    other = 1 - core
    a, b = y * other + z * core, z * other + y * core
    twin = (row + 1 - 2 * core, col)

    def at_x(d):
        return (row, (x + d) % nx * n + z)

    def at_z(d):
        return (row, x * n + (z + d) % n)

    def at_y(d):
        return ((y + d) % n * 2 + core, col)

    def at_a(d):
        return (((y + d * other) % n) * 2 + core, x * n + (z + d * core) % n)

    def at_b(d):
        return (((y + d * core) % n) * 2 + core, x * n + (z + d * other) % n)

    barrier = pltpu.get_barrier_semaphore()
    peers = [at_x(d) for d in range(1, nx)] + [f(d) for f in (at_z, at_y) for d in range(1, n)] + [twin]
    for peer in peers:
        pl.semaphore_signal(barrier, inc=1, device_id=peer, device_id_type=MESH)

    def copy(src, dst, send, recv, peer):
        return pltpu.make_async_remote_copy(
            src_ref=src, dst_ref=dst, send_sem=send, recv_sem=recv, device_id=peer, device_id_type=MESH)

    half = x_ref.shape[1] // 2
    wide = half // nx

    def slices(to):
        lanes = pl.multiple_of(to * wide, wide)
        return [x_ref.at[:, pl.ds(lanes, wide)], x_ref.at[:, pl.ds(half + lanes, wide)], u_ref, v_ref]

    def slots(d):
        return [xs.at[d, 0], xs.at[d, 1], fs.at[d, 0], fs.at[d, 1]]

    own = [pltpu.make_async_copy(s, t, own_s.at[i]) for i, (s, t) in enumerate(zip(slices(x), slots(0)))]
    for c in own:
        c.start()
    pl.semaphore_wait(barrier, len(peers))

    sent = []

    def go(c):
        c.start()
        sent.append(c)

    def finish():
        for c in sent:
            c.wait_send()

    for d in range(1, nx):
        for i, (s, t) in enumerate(zip(slices((x + d) % nx), slots(d))):
            go(copy(s, t, xs_s.at[d - 1, i], xs_r.at[d - 1, i], at_x(d)))
    for c in own:
        c.wait()

    def product(d):
        f = fs[d].reshape(-1, fs.shape[-1])
        zero = jnp.zeros_like(f)
        over = (((0,), (1,)), ((), ()))
        return lax.dot_general(xs[d, 0], jnp.concatenate([f, zero], axis=0), over, preferred_element_type=F32) + \
            lax.dot_general(xs[d, 1], jnp.concatenate([zero, f], axis=0), over, preferred_element_type=F32)

    total = product(0)
    for d in range(1, nx):
        for i, (s, t) in enumerate(zip(slices(x), slots(d))):
            copy(s, t, xs_s.at[d - 1, i], xs_r.at[d - 1, i], at_x(d)).wait_recv()
        total = total + product(d)
    sumx[...] = total.reshape(sumx.shape)

    for d in range(1, n):
        go(copy(sumx.at[(z + d) % n], rz.at[d - 1], rz_s.at[d - 1], rz_r.at[d - 1], at_z(d)))
    tile = sumx[z]
    for d in range(1, n):
        copy(sumx.at[z], rz.at[d - 1], rz_s.at[d - 1], rz_r.at[d - 1], at_z(d)).wait_recv()
        tile = tile + rz[d - 1]
    mine[...] = tile.astype(BF16)

    keep = pltpu.make_async_copy(mine, tab.at[core, b, x, a], own_s.at[4])
    keep.start()
    for d in range(1, n):
        go(copy(mine, tab.at[core, b, x, a], aa_s.at[d - 1], aa_r.at[d - 1], at_a(d)))
    keep.wait()
    for d in range(1, n):
        copy(mine, tab.at[core, b, x, (a + n - d) % n], aa_s.at[d - 1], aa_r.at[d - 1], at_a(d)).wait_recv()

    def piece(away, e):
        return tab.at[core, (b + n - away) % n, (x + nx - e) % nx]

    for d in range(1, nx):
        go(copy(piece(0, 0), piece(0, 0), ax_s.at[d - 1], ax_r.at[d - 1], at_x(d)))

    def pass_on(k, e):
        go(copy(piece(k, e), piece(k, e), tw_s.at[k, e], tw_r.at[k, e], twin))

    for e in range(nx):
        if e:
            copy(piece(0, e), piece(0, e), ax_s.at[e - 1], ax_r.at[e - 1], at_x(e)).wait_recv()
        for d in (1, n - 1, 2, n - 2):
            go(copy(piece(0, e), piece(0, e), bb_s.at[d, e], bb_r.at[d, e], at_b(d)))
        pass_on(0, e)

    def land(k, e):
        copy(piece(k, e), piece(k, e), bb_s.at[k, e], bb_r.at[k, e], at_b(k)).wait_recv()

    for e in range(nx):
        for k, onward in ((2, (1, 2) if e % 2 == 0 else (1,)), (n - 2, (n - 1,) if e % 2 == 0 else (n - 1, n - 2))):
            land(k, e)
            for d in onward:
                go(copy(piece(k, e), piece(k, e), bb_s.at[(k + d) % n, e], bb_r.at[(k + d) % n, e], at_b(d)))
            pass_on(k, e)
        for k in (1, n - 1):
            land(k, e)
            pass_on(k, e)
    for e in range(nx):
        for k in (3, n - 3, 4):
            land(k, e)
            pass_on(k, e)
    theirs = z * core + y * other
    for k in range(n):
        for e in range(nx):
            ref = tab.at[other, (theirs + n - k) % n, (x + nx - e) % nx]
            copy(ref, ref, tw_s.at[k, e], tw_r.at[k, e], twin).wait_recv()
    finish()


def share(nx, n, vectors, u, v):
    depth, rows = vectors.shape
    block = rows // 2 // (nx * n)
    dma = pltpu.SemaphoreType.DMA
    tab = (2, n, nx, n, block, 128)
    hbm = pl.BlockSpec(memory_space=pltpu.MemorySpace.HBM)
    pairs = []
    for shape in ((nx - 1, 4), (n - 1,), (n - 1,), (nx - 1,), (n, nx), (n, nx)):
        pairs += [dma(shape), dma(shape)]
    return pl.pallas_call(
        functools.partial(share_kernel, nx, n),
        out_shape=jax.ShapeDtypeStruct(tab, BF16),
        in_specs=[hbm] * 3,
        out_specs=pl.BlockSpec(memory_space=pl.ANY),
        scratch_shapes=[
            pltpu.VMEM((nx, 2, depth, rows // 2 // nx), BF16),
            pltpu.VMEM((nx, 2) + u.shape, BF16),
            pltpu.VMEM((n, block, 128), F32),
            pltpu.VMEM((n - 1, block, 128), F32),
            pltpu.VMEM((block, 128), BF16),
            dma((5,)),
        ] + pairs,
        compiler_params=pltpu.CompilerParams(collective_id=0, has_side_effects=True, vmem_limit_bytes=8 << 20),
    )(vectors, u, v)


def in_hbm(t):
    return pltpu.with_memory_space_constraint(t, pltpu.MemorySpace.HBM)


def body(outcome_vectors, u_factor, v_factor, outcome_index):
    table = share(4, 8, in_hbm(outcome_vectors.T), in_hbm(u_factor), in_hbm(v_factor))
    return local_part(lambda: (lax.axis_index("row"), lax.axis_index("col")))(outcome_index, table)


def solution(mesh):
    placed = (P("row", "col"), P(None, "col"), P(None, "col"), P())
    return jax.shard_map(
        body, mesh=mesh, in_specs=placed, out_specs=P("row", "col"), check_vma=False
    )
```

```python
import functools

import jax
import jax.numpy as jnp
from jax import lax
from jax.experimental import pallas as pl
from jax.experimental.pallas import tpu as pltpu
from jax.sharding import PartitionSpec as P

F32 = jnp.float32
HI = lax.Precision.HIGHEST
NT = (((1,), (1,)), ((), ()))


def spread(x, j):
    return jnp.take_along_axis(x, jnp.full((8, 128), j, jnp.int32), axis=1)


def row_of(x, i):
    return jnp.broadcast_to(x[i : i + 1, :], (8, 128))


def factor_block(load, store, lanes, subs, hook):
    A = [load(t) for t in range(16)]
    for t in range(16):
        j0 = 8 * t
        inside = (lanes >= j0) & (lanes < j0 + 8)
        C = [spread(A[t], j0 + i) for i in range(8)]
        R = A[t]
        piv = jnp.zeros((8, 128), F32)
        rows, outer = {}, []
        for i in range(8):
            p = row_of(C[i], i)
            ip = 1.0 / p
            piv = jnp.where(subs == i, p, piv)
            Ri = jnp.where(lanes == j0 + i, 1.0, row_of(R, i)) * ip
            for l in range(i + 1, 8):
                rows[i, l] = row_of(C[l], i) * ip
            m = jnp.where(subs > i, C[i], 0.0)
            R = jnp.where((subs > i) & (lanes == j0 + i), 0.0, R) - m * Ri
            for l in range(i + 1, 8):
                C[l] = C[l] - m * rows[i, l]
            outer.append(jnp.where((lanes > j0 + i) & (lanes < j0 + 8), 0.0, Ri))
        rs = lax.rsqrt(piv)
        store(t, jnp.where(lanes < j0 + subs, R * rs, jnp.where(lanes == j0 + subs, rs, 0.0)))
        for s in range(t + 1, 16):
            D = [spread(A[s], j0 + i) for i in range(8)]
            q = jnp.where(inside, 0.0, A[s])
            for i in range(8):
                q = q - D[i] * outer[i]
                for l in range(i + 1, 8):
                    D[l] = D[l] - D[i] * rows[i, l]
            A[s] = q
        hook(t)


def split(x):
    high = x.astype(jnp.bfloat16)
    return high, (x - high.astype(F32)).astype(jnp.bfloat16)


def dot(a, b):
    return lax.dot_general(a, b, NT, preferred_element_type=F32)


def three(a, b):
    return dot(a[0], b[0]) + (dot(a[0], b[1]) + dot(a[1], b[0]))


def kernel(rc, idx_hbm, tab_ref, out_hbm, out_ref, idx_ref, idx_sem, out_sem, t2, g32, gu, gv, sx, inv_ref, ch, cl, invh, invl, lh, ll):
    r, c = rc() if callable(rc) else rc
    runs = [
        pltpu.make_async_copy(idx_hbm.at[pl.ds(pl.multiple_of(first, 1024), 1024)], idx_ref.at[pl.ds(1024 * i, 1024)], idx_sem.at[i])
        for i, first in enumerate((0, c // 2 * 1024, r * 1024))
    ]
    for run in runs:
        run.start()
    lanes = lax.broadcasted_iota(jnp.int32, (8, 128), 1)
    subs = lax.broadcasted_iota(jnp.int32, (8, 128), 0)

    def unpack(b, _):
        for core in range(2):
            for x in range(4):
                for a in range(8):
                    y, z = (a, b) if core == 0 else (b, a)
                    tile = tab_ref[core, b, x, a].astype(F32)
                    dst = pl.multiple_of((y * 2 + core) * 1024 + (x * 8 + z) * 16, 16)
                    t2[pl.ds(dst, 16), :] = tile
                    t2[pl.ds(dst + 512, 16), :] = pltpu.roll(tile, 64, 1)
        return 0

    lax.fori_loop(0, 8, unpack, 0)

    def pick(n, base, dst):
        def body(i, _):
            for q in range(16):
                j = i * 16 + q
                g32[pl.ds(dst + j, 1), :] = t2[pl.ds(idx_ref[base + j], 1), :]
            return 0
        lax.fori_loop(0, n // 16, body, 0)

    for run in runs:
        run.wait()
    pick(512, 0, 0)
    pick(512, 1024 + c % 2 * 512, 512)
    pick(1024, 2048, 1024)
    wide = lax.broadcasted_iota(jnp.int32, (256, 128), 1)

    def masks(i, _):
        rows = pl.ds(pl.multiple_of(i * 256, 256), 256)
        g = g32[rows, :]
        gu[rows, :] = jnp.where(wide < 32, g, 0.0).astype(jnp.bfloat16)
        gv[rows, :] = jnp.where((wide >= 32) & (wide < 64), g, 0.0).astype(jnp.bfloat16)
        return 0

    lax.fori_loop(0, 8, masks, 0)

    def gram(rows, cols):
        return dot(gu[rows, :], gu[cols, :]) * dot(gv[rows, :], gv[cols, :])

    il = lax.broadcasted_iota(jnp.int32, (256, 512), 0)
    ic = lax.broadcasted_iota(jnp.int32, (256, 512), 1)

    def columns(i):
        rows = pl.ds(i * 256, 256)
        first = i * 256 if i < 2 else (c * 512 + (i - 2) * 256 if i < 4 else r * 1024 + (i - 4) * 256)
        sx[rows, :] = gram(rows, pl.ds(0, 512)) + jnp.where(il + first == ic, 1.0, 0.0)

    def full(a, b):
        return lax.dot_general(a, b, NT, precision=HI, preferred_element_type=F32)

    def solve(k, rows):
        cols = pl.ds(k * 128, 128)
        b = three(split(sx[rows, cols]), (invh[k], invl[k]))
        sx[rows, cols] = b
        if k < 3:
            rest = pl.ds(k * 128 + 128, 384 - k * 128)
            sx[rows, rest] = sx[rows, rest] - three(split(b), (lh[rest, cols], ll[rest, cols]))

    def block(i):
        grow = il + (r * 1024 + i * 256)
        return pl.ds(i * 256, 256), pl.ds(1024 + i * 256, 256), grow

    def fill(i):
        dst, rows, grow = block(i)
        out_ref[dst, :] = gram(rows, pl.ds(512, 512)) + jnp.where(grow == ic + c * 512, 1.0, 0.0)

    def product(rows, keep, cols):
        return three(split(jnp.where(keep, sx[rows, cols], 0.0)), (ch[:, cols], cl[:, cols]))

    def first_half(i):
        dst, rows, grow = block(i)
        out_ref[dst, :] = out_ref[dst, :] - product(rows, grow[:, :256] >= 256, pl.ds(0, 256))

    def hook(k, t):
        if k == 0:
            if t < 6:
                columns(2 + t)
            elif t < 10:
                fill(t - 6)
        elif t < 12:
            solve(k - 1, pl.ds(512 + 128 * t, 128))
        elif k == 3:
            if t == 12:
                ch[:, :256], cl[:, :256] = split(sx[pl.ds(512, 512), pl.ds(0, 256)])
            first_half(t - 12)

    columns(0)
    columns(1)

    for k in range(4):
        cols = pl.ds(k * 128, 128)
        factor_block(
            lambda t: sx[pl.ds(k * 128 + 8 * t, 8), cols],
            lambda t, v: inv_ref.__setitem__((k, pl.ds(8 * t, 8), slice(None)), v),
            lanes, subs, functools.partial(hook, k),
        )
        invh[k], invl[k] = split(inv_ref[k])
        if k < 3:
            rows = pl.ds(k * 128, 512 - k * 128)
            b = full(sx[rows, cols], inv_ref[k])
            sx[rows, cols] = b
            rest = pl.ds(k * 128 + 128, 384 - k * 128)
            sx[rest, rest] = sx[rest, rest] - full(b[128:], b[128:])
            lh[rest, cols], ll[rest, cols] = split(b[128:])
    for i in range(6):
        solve(3, pl.ds(512 + 256 * i, 256))
    ch[:, 256:], cl[:, 256:] = split(sx[pl.ds(512, 512), pl.ds(256, 256)])

    writes = []
    for i in range(4):
        dst, rows, grow = block(i)
        s, b = out_ref[dst, :], sx[rows, :]
        lead = jnp.where(ic <= grow, b, jnp.where((grow < 256) & (ic >= 256), s, 0.0))
        panel = jnp.where(grow < 512, lead, b)
        trailing = s - product(rows, grow[:, :256] >= 512, pl.ds(256, 256))
        out_ref[dst, :] = jnp.where(c == 0, panel, trailing)
        writes.append(pltpu.make_async_copy(out_ref.at[dst], out_hbm.at[dst], out_sem.at[i]))
        writes[-1].start()
    for write in writes:
        write.wait()


def local_part(rc):
    def f(idx, tab):
        return pl.pallas_call(
            functools.partial(kernel, rc),
            out_shape=jax.ShapeDtypeStruct((1024, 512), F32),
            in_specs=[pl.BlockSpec(memory_space=pl.ANY), pl.BlockSpec(memory_space=pltpu.VMEM)],
            out_specs=pl.BlockSpec(memory_space=pl.ANY),
            scratch_shapes=[
                pltpu.VMEM((1024, 512), F32),
                pltpu.SMEM((3072,), jnp.int32),
                pltpu.SemaphoreType.DMA((3,)),
                pltpu.SemaphoreType.DMA((4,)),
                pltpu.VMEM((16384, 128), F32),
                pltpu.VMEM((2048, 128), F32),
                pltpu.VMEM((2048, 128), jnp.bfloat16),
                pltpu.VMEM((2048, 128), jnp.bfloat16),
                pltpu.VMEM((2048, 512), F32),
                pltpu.VMEM((4, 128, 128), F32),
                pltpu.VMEM((512, 512), jnp.bfloat16),
                pltpu.VMEM((512, 512), jnp.bfloat16),
                pltpu.VMEM((4, 128, 128), jnp.bfloat16),
                pltpu.VMEM((4, 128, 128), jnp.bfloat16),
                pltpu.VMEM((512, 512), jnp.bfloat16),
                pltpu.VMEM((512, 512), jnp.bfloat16),
            ],
            compiler_params=pltpu.CompilerParams(vmem_limit_bytes=24 << 20),
        )(idx, tab)
    return f


MESH = pl.DeviceIdType.MESH
BF16 = jnp.bfloat16

def share_kernel(nx, n, x_ref, u_ref, v_ref, tab, xs, fs, sumx, rz, mine,
                 own_s, xs_s, xs_r, rz_s, rz_r, aa_s, aa_r, ax_s, ax_r, bb_s, bb_r, tw_s, tw_r):
    row, col = lax.axis_index("row"), lax.axis_index("col")
    y, core = row // 2, row % 2
    x, z = col // n, col % n
    other = 1 - core
    a, b = y * other + z * core, z * other + y * core
    twin = (row + 1 - 2 * core, col)

    def at_x(d):
        return (row, (x + d) % nx * n + z)

    def at_z(d):
        return (row, x * n + (z + d) % n)

    def at_y(d):
        return ((y + d) % n * 2 + core, col)

    def at_a(d):
        return (((y + d * other) % n) * 2 + core, x * n + (z + d * core) % n)

    def at_b(d):
        return (((y + d * core) % n) * 2 + core, x * n + (z + d * other) % n)

    barrier = pltpu.get_barrier_semaphore()
    peers = [at_x(d) for d in range(1, nx)] + [f(d) for f in (at_z, at_y) for d in range(1, n)] + [twin]
    for peer in peers:
        pl.semaphore_signal(barrier, inc=1, device_id=peer, device_id_type=MESH)

    def copy(src, dst, send, recv, peer):
        return pltpu.make_async_remote_copy(
            src_ref=src, dst_ref=dst, send_sem=send, recv_sem=recv, device_id=peer, device_id_type=MESH)

    half = x_ref.shape[1] // 2
    wide = half // nx

    def slices(to):
        lanes = pl.multiple_of(to * wide, wide)
        return [x_ref.at[:, pl.ds(lanes, wide)], x_ref.at[:, pl.ds(half + lanes, wide)], u_ref, v_ref]

    def slots(d):
        return [xs.at[d, 0], xs.at[d, 1], fs.at[d, 0], fs.at[d, 1]]

    own = [pltpu.make_async_copy(s, t, own_s.at[i]) for i, (s, t) in enumerate(zip(slices(x), slots(0)))]
    for c in own:
        c.start()
    pl.semaphore_wait(barrier, len(peers))

    sent = []

    def go(c):
        c.start()
        sent.append(c)

    def finish():
        for c in sent:
            c.wait_send()

    for d in range(1, nx):
        for i, (s, t) in enumerate(zip(slices((x + d) % nx), slots(d))):
            go(copy(s, t, xs_s.at[d - 1, i], xs_r.at[d - 1, i], at_x(d)))
    for c in own:
        c.wait()

    def product(d):
        f = fs[d].reshape(-1, fs.shape[-1])
        zero = jnp.zeros_like(f)
        over = (((0,), (1,)), ((), ()))
        return lax.dot_general(xs[d, 0], jnp.concatenate([f, zero], axis=0), over, preferred_element_type=F32) + \
            lax.dot_general(xs[d, 1], jnp.concatenate([zero, f], axis=0), over, preferred_element_type=F32)

    total = product(0)
    for d in range(1, nx):
        for i, (s, t) in enumerate(zip(slices(x), slots(d))):
            copy(s, t, xs_s.at[d - 1, i], xs_r.at[d - 1, i], at_x(d)).wait_recv()
        total = total + product(d)
    sumx[...] = total.reshape(sumx.shape)

    for d in range(1, n):
        go(copy(sumx.at[(z + d) % n], rz.at[d - 1], rz_s.at[d - 1], rz_r.at[d - 1], at_z(d)))
    tile = sumx[z]
    for d in range(1, n):
        copy(sumx.at[z], rz.at[d - 1], rz_s.at[d - 1], rz_r.at[d - 1], at_z(d)).wait_recv()
        tile = tile + rz[d - 1]
    mine[...] = tile.astype(BF16)

    keep = pltpu.make_async_copy(mine, tab.at[core, b, x, a], own_s.at[4])
    keep.start()
    for d in range(1, n):
        go(copy(mine, tab.at[core, b, x, a], aa_s.at[d - 1], aa_r.at[d - 1], at_a(d)))
    keep.wait()
    for d in range(1, n):
        copy(mine, tab.at[core, b, x, (a + n - d) % n], aa_s.at[d - 1], aa_r.at[d - 1], at_a(d)).wait_recv()

    def piece(away, e):
        return tab.at[core, (b + n - away) % n, (x + nx - e) % nx]

    for d in range(1, nx):
        go(copy(piece(0, 0), piece(0, 0), ax_s.at[d - 1], ax_r.at[d - 1], at_x(d)))

    def pass_on(k, e):
        go(copy(piece(k, e), piece(k, e), tw_s.at[k, e], tw_r.at[k, e], twin))

    for e in range(nx):
        if e:
            copy(piece(0, e), piece(0, e), ax_s.at[e - 1], ax_r.at[e - 1], at_x(e)).wait_recv()
        for d in (1, n - 1, 2, n - 2):
            go(copy(piece(0, e), piece(0, e), bb_s.at[d, e], bb_r.at[d, e], at_b(d)))
        pass_on(0, e)

    def land(k, e):
        copy(piece(k, e), piece(k, e), bb_s.at[k, e], bb_r.at[k, e], at_b(k)).wait_recv()

    for e in range(nx):
        for k, onward in ((2, (1, 2) if e % 2 == 0 else (1,)), (n - 2, (n - 1,) if e % 2 == 0 else (n - 1, n - 2))):
            land(k, e)
            for d in onward:
                go(copy(piece(k, e), piece(k, e), bb_s.at[(k + d) % n, e], bb_r.at[(k + d) % n, e], at_b(d)))
            pass_on(k, e)
        for k in (1, n - 1):
            land(k, e)
            pass_on(k, e)
    for e in range(nx):
        for k in (3, n - 3, 4):
            land(k, e)
            pass_on(k, e)
    theirs = z * core + y * other
    for k in range(n):
        for e in range(nx):
            ref = tab.at[other, (theirs + n - k) % n, (x + nx - e) % nx]
            copy(ref, ref, tw_s.at[k, e], tw_r.at[k, e], twin).wait_recv()
    finish()


def share(nx, n, vectors, u, v):
    depth, rows = vectors.shape
    block = rows // 2 // (nx * n)
    dma = pltpu.SemaphoreType.DMA
    tab = (2, n, nx, n, block, 128)
    hbm = pl.BlockSpec(memory_space=pltpu.MemorySpace.HBM)
    pairs = []
    for shape in ((nx - 1, 4), (n - 1,), (n - 1,), (nx - 1,), (n, nx), (n, nx)):
        pairs += [dma(shape), dma(shape)]
    return pl.pallas_call(
        functools.partial(share_kernel, nx, n),
        out_shape=jax.ShapeDtypeStruct(tab, BF16),
        in_specs=[hbm] * 3,
        out_specs=pl.BlockSpec(memory_space=pl.ANY),
        scratch_shapes=[
            pltpu.VMEM((nx, 2, depth, rows // 2 // nx), BF16),
            pltpu.VMEM((nx, 2) + u.shape, BF16),
            pltpu.VMEM((n, block, 128), F32),
            pltpu.VMEM((n - 1, block, 128), F32),
            pltpu.VMEM((block, 128), BF16),
            dma((5,)),
        ] + pairs,
        compiler_params=pltpu.CompilerParams(collective_id=0, has_side_effects=True, vmem_limit_bytes=8 << 20),
    )(vectors, u, v)


def in_hbm(t):
    return pltpu.with_memory_space_constraint(t, pltpu.MemorySpace.HBM)


def body(outcome_vectors, u_factor, v_factor, outcome_index):
    table = share(4, 8, in_hbm(outcome_vectors.T), in_hbm(u_factor), in_hbm(v_factor))
    return local_part(lambda: (lax.axis_index("row"), lax.axis_index("col")))(outcome_index, table)


def solution(mesh):
    placed = (P("row", "col"), P(None, "col"), P(None, "col"), P())
    return jax.shard_map(
        body, mesh=mesh, in_specs=placed, out_specs=P("row", "col"), check_vma=False
    )
```

```python
import functools

import jax
import jax.numpy as jnp
from jax import lax
from jax.experimental import pallas as pl
from jax.experimental.pallas import tpu as pltpu
from jax.sharding import PartitionSpec as P

F32 = jnp.float32
HI = lax.Precision.HIGHEST
NT = (((1,), (1,)), ((), ()))


def spread(x, j):
    return jnp.take_along_axis(x, jnp.full((8, 128), j, jnp.int32), axis=1)


def row_of(x, i):
    return jnp.broadcast_to(x[i : i + 1, :], (8, 128))


def factor_block(load, store, lanes, subs, hook):
    A = [load(t) for t in range(16)]
    for t in range(16):
        j0 = 8 * t
        inside = (lanes >= j0) & (lanes < j0 + 8)
        C = [spread(A[t], j0 + i) for i in range(8)]
        R = A[t]
        piv = jnp.zeros((8, 128), F32)
        rows, outer = {}, []
        for i in range(8):
            p = row_of(C[i], i)
            ip = 1.0 / p
            piv = jnp.where(subs == i, p, piv)
            Ri = jnp.where(lanes == j0 + i, 1.0, row_of(R, i)) * ip
            for l in range(i + 1, 8):
                rows[i, l] = row_of(C[l], i) * ip
            m = jnp.where(subs > i, C[i], 0.0)
            R = jnp.where((subs > i) & (lanes == j0 + i), 0.0, R) - m * Ri
            for l in range(i + 1, 8):
                C[l] = C[l] - m * rows[i, l]
            outer.append(jnp.where((lanes > j0 + i) & (lanes < j0 + 8), 0.0, Ri))
        rs = lax.rsqrt(piv)
        store(t, jnp.where(lanes < j0 + subs, R * rs, jnp.where(lanes == j0 + subs, rs, 0.0)))
        for s in range(t + 1, 16):
            D = [spread(A[s], j0 + i) for i in range(8)]
            q = jnp.where(inside, 0.0, A[s])
            for i in range(8):
                q = q - D[i] * outer[i]
                for l in range(i + 1, 8):
                    D[l] = D[l] - D[i] * rows[i, l]
            A[s] = q
        hook(t)


def split(x):
    high = x.astype(jnp.bfloat16)
    return high, (x - high.astype(F32)).astype(jnp.bfloat16)


def dot(a, b):
    return lax.dot_general(a, b, NT, preferred_element_type=F32)


def three(a, b):
    return dot(a[0], b[0]) + (dot(a[0], b[1]) + dot(a[1], b[0]))


def kernel(rc, idx_hbm, tab_ref, out_hbm, out_ref, idx_ref, idx_sem, out_sem, t2, g32, gu, gv, sx, inv_ref, ch, cl, invh, invl, lh, ll):
    r, c = rc() if callable(rc) else rc
    runs = [
        pltpu.make_async_copy(idx_hbm.at[pl.ds(pl.multiple_of(first, 1024), 1024)], idx_ref.at[pl.ds(1024 * i, 1024)], idx_sem.at[i])
        for i, first in enumerate((0, c // 2 * 1024, r * 1024))
    ]
    for run in runs:
        run.start()
    lanes = lax.broadcasted_iota(jnp.int32, (8, 128), 1)
    subs = lax.broadcasted_iota(jnp.int32, (8, 128), 0)

    def unpack(b, _):
        for core in range(2):
            for x in range(4):
                for a in range(8):
                    y, z = (a, b) if core == 0 else (b, a)
                    tile = tab_ref[core, b, x, a].astype(F32)
                    dst = pl.multiple_of((y * 2 + core) * 1024 + (x * 8 + z) * 16, 16)
                    t2[pl.ds(dst, 16), :] = tile
                    t2[pl.ds(dst + 512, 16), :] = pltpu.roll(tile, 64, 1)
        return 0

    lax.fori_loop(0, 8, unpack, 0)

    def pick(n, base, dst):
        def body(i, _):
            for q in range(16):
                j = i * 16 + q
                g32[pl.ds(dst + j, 1), :] = t2[pl.ds(idx_ref[base + j], 1), :]
            return 0
        lax.fori_loop(0, n // 16, body, 0)

    for run in runs:
        run.wait()
    pick(512, 0, 0)
    pick(512, 1024 + c % 2 * 512, 512)
    pick(1024, 2048, 1024)
    wide = lax.broadcasted_iota(jnp.int32, (256, 128), 1)

    def masks(i, _):
        rows = pl.ds(pl.multiple_of(i * 256, 256), 256)
        g = g32[rows, :]
        gu[rows, :] = jnp.where(wide < 32, g, 0.0).astype(jnp.bfloat16)
        gv[rows, :] = jnp.where((wide >= 32) & (wide < 64), g, 0.0).astype(jnp.bfloat16)
        return 0

    lax.fori_loop(0, 8, masks, 0)

    def gram(rows, cols):
        return dot(gu[rows, :], gu[cols, :]) * dot(gv[rows, :], gv[cols, :])

    il = lax.broadcasted_iota(jnp.int32, (256, 512), 0)
    ic = lax.broadcasted_iota(jnp.int32, (256, 512), 1)

    def columns(i):
        rows = pl.ds(i * 256, 256)
        first = i * 256 if i < 2 else (c * 512 + (i - 2) * 256 if i < 4 else r * 1024 + (i - 4) * 256)
        sx[rows, :] = gram(rows, pl.ds(0, 512)) + jnp.where(il + first == ic, 1.0, 0.0)

    def full(a, b):
        return lax.dot_general(a, b, NT, precision=HI, preferred_element_type=F32)

    def solve(k, rows):
        cols = pl.ds(k * 128, 128)
        b = three(split(sx[rows, cols]), (invh[k], invl[k]))
        sx[rows, cols] = b
        if k < 3:
            rest = pl.ds(k * 128 + 128, 384 - k * 128)
            sx[rows, rest] = sx[rows, rest] - three(split(b), (lh[rest, cols], ll[rest, cols]))

    def block(i):
        grow = il + (r * 1024 + i * 256)
        return pl.ds(i * 256, 256), pl.ds(1024 + i * 256, 256), grow

    def fill(i):
        dst, rows, grow = block(i)
        out_ref[dst, :] = gram(rows, pl.ds(512, 512)) + jnp.where(grow == ic + c * 512, 1.0, 0.0)

    def product(rows, keep, cols):
        return three(split(jnp.where(keep, sx[rows, cols], 0.0)), (ch[:, cols], cl[:, cols]))

    def first_half(i):
        dst, rows, grow = block(i)
        out_ref[dst, :] = out_ref[dst, :] - product(rows, grow[:, :256] >= 256, pl.ds(0, 256))

    def hook(k, t):
        if k == 0:
            if t < 6:
                columns(2 + t)
            elif t < 10:
                fill(t - 6)
        elif t < 12:
            solve(k - 1, pl.ds(512 + 128 * t, 128))
        elif k == 3:
            if t == 12:
                ch[:, :256], cl[:, :256] = split(sx[pl.ds(512, 512), pl.ds(0, 256)])
            first_half(t - 12)

    columns(0)
    columns(1)

    for k in range(4):
        cols = pl.ds(k * 128, 128)
        factor_block(
            lambda t: sx[pl.ds(k * 128 + 8 * t, 8), cols],
            lambda t, v: inv_ref.__setitem__((k, pl.ds(8 * t, 8), slice(None)), v),
            lanes, subs, functools.partial(hook, k),
        )
        invh[k], invl[k] = split(inv_ref[k])
        if k < 3:
            rows = pl.ds(k * 128, 512 - k * 128)
            b = full(sx[rows, cols], inv_ref[k])
            sx[rows, cols] = b
            rest = pl.ds(k * 128 + 128, 384 - k * 128)
            sx[rest, rest] = sx[rest, rest] - full(b[128:], b[128:])
            lh[rest, cols], ll[rest, cols] = split(b[128:])
    for i in range(6):
        solve(3, pl.ds(512 + 256 * i, 256))
    ch[:, 256:], cl[:, 256:] = split(sx[pl.ds(512, 512), pl.ds(256, 256)])

    writes = []
    for i in range(4):
        dst, rows, grow = block(i)
        s, b = out_ref[dst, :], sx[rows, :]
        lead = jnp.where(ic <= grow, b, jnp.where((grow < 256) & (ic >= 256), s, 0.0))
        panel = jnp.where(grow < 512, lead, b)
        trailing = s - product(rows, grow[:, :256] >= 512, pl.ds(256, 256))
        out_ref[dst, :] = jnp.where(c == 0, panel, trailing)
        writes.append(pltpu.make_async_copy(out_ref.at[dst], out_hbm.at[dst], out_sem.at[i]))
        writes[-1].start()
    for write in writes:
        write.wait()


def local_part(rc):
    def f(idx, tab):
        return pl.pallas_call(
            functools.partial(kernel, rc),
            out_shape=jax.ShapeDtypeStruct((1024, 512), F32),
            in_specs=[pl.BlockSpec(memory_space=pl.ANY), pl.BlockSpec(memory_space=pltpu.VMEM)],
            out_specs=pl.BlockSpec(memory_space=pl.ANY),
            scratch_shapes=[
                pltpu.VMEM((1024, 512), F32),
                pltpu.SMEM((3072,), jnp.int32),
                pltpu.SemaphoreType.DMA((3,)),
                pltpu.SemaphoreType.DMA((4,)),
                pltpu.VMEM((16384, 128), F32),
                pltpu.VMEM((2048, 128), F32),
                pltpu.VMEM((2048, 128), jnp.bfloat16),
                pltpu.VMEM((2048, 128), jnp.bfloat16),
                pltpu.VMEM((2048, 512), F32),
                pltpu.VMEM((4, 128, 128), F32),
                pltpu.VMEM((512, 512), jnp.bfloat16),
                pltpu.VMEM((512, 512), jnp.bfloat16),
                pltpu.VMEM((4, 128, 128), jnp.bfloat16),
                pltpu.VMEM((4, 128, 128), jnp.bfloat16),
                pltpu.VMEM((512, 512), jnp.bfloat16),
                pltpu.VMEM((512, 512), jnp.bfloat16),
            ],
            compiler_params=pltpu.CompilerParams(vmem_limit_bytes=24 << 20),
        )(idx, tab)
    return f


MESH = pl.DeviceIdType.MESH
BF16 = jnp.bfloat16

def share_kernel(nx, n, x_ref, u_ref, v_ref, tab, xs, fs, sumx, rz, mine,
                 own_s, xs_s, xs_r, rz_s, rz_r, aa_s, aa_r, ax_s, ax_r, bb_s, bb_r, tw_s, tw_r):
    row, col = lax.axis_index("row"), lax.axis_index("col")
    y, core = row // 2, row % 2
    x, z = col // n, col % n
    other = 1 - core
    a, b = y * other + z * core, z * other + y * core
    twin = (row + 1 - 2 * core, col)

    def at_x(d):
        return (row, (x + d) % nx * n + z)

    def at_z(d):
        return (row, x * n + (z + d) % n)

    def at_y(d):
        return ((y + d) % n * 2 + core, col)

    def at_a(d):
        return (((y + d * other) % n) * 2 + core, x * n + (z + d * core) % n)

    def at_b(d):
        return (((y + d * core) % n) * 2 + core, x * n + (z + d * other) % n)

    barrier = pltpu.get_barrier_semaphore()
    peers = [at_x(d) for d in range(1, nx)] + [f(d) for f in (at_z, at_y) for d in range(1, n)] + [twin]
    for peer in peers:
        pl.semaphore_signal(barrier, inc=1, device_id=peer, device_id_type=MESH)

    def copy(src, dst, send, recv, peer):
        return pltpu.make_async_remote_copy(
            src_ref=src, dst_ref=dst, send_sem=send, recv_sem=recv, device_id=peer, device_id_type=MESH)

    half = x_ref.shape[1] // 2
    wide = half // nx

    def slices(to):
        lanes = pl.multiple_of(to * wide, wide)
        return [x_ref.at[:, pl.ds(lanes, wide)], x_ref.at[:, pl.ds(half + lanes, wide)], u_ref, v_ref]

    def slots(d):
        return [xs.at[d, 0], xs.at[d, 1], fs.at[d, 0], fs.at[d, 1]]

    own = [pltpu.make_async_copy(s, t, own_s.at[i]) for i, (s, t) in enumerate(zip(slices(x), slots(0)))]
    for c in own:
        c.start()
    pl.semaphore_wait(barrier, len(peers))

    sent = []

    def go(c):
        c.start()
        sent.append(c)

    def finish():
        for c in sent:
            c.wait_send()

    for d in range(1, nx):
        for i, (s, t) in enumerate(zip(slices((x + d) % nx), slots(d))):
            go(copy(s, t, xs_s.at[d - 1, i], xs_r.at[d - 1, i], at_x(d)))
    for c in own:
        c.wait()

    def product(d):
        f = fs[d].reshape(-1, fs.shape[-1])
        zero = jnp.zeros_like(f)
        over = (((0,), (1,)), ((), ()))
        return lax.dot_general(xs[d, 0], jnp.concatenate([f, zero], axis=0), over, preferred_element_type=F32) + \
            lax.dot_general(xs[d, 1], jnp.concatenate([zero, f], axis=0), over, preferred_element_type=F32)

    total = product(0)
    for d in range(1, nx):
        for i, (s, t) in enumerate(zip(slices(x), slots(d))):
            copy(s, t, xs_s.at[d - 1, i], xs_r.at[d - 1, i], at_x(d)).wait_recv()
        total = total + product(d)
    sumx[...] = total.reshape(sumx.shape)

    for d in range(1, n):
        go(copy(sumx.at[(z + d) % n], rz.at[d - 1], rz_s.at[d - 1], rz_r.at[d - 1], at_z(d)))
    tile = sumx[z]
    for d in range(1, n):
        copy(sumx.at[z], rz.at[d - 1], rz_s.at[d - 1], rz_r.at[d - 1], at_z(d)).wait_recv()
        tile = tile + rz[d - 1]
    mine[...] = tile.astype(BF16)

    keep = pltpu.make_async_copy(mine, tab.at[core, b, x, a], own_s.at[4])
    keep.start()
    for d in range(1, n):
        go(copy(mine, tab.at[core, b, x, a], aa_s.at[d - 1], aa_r.at[d - 1], at_a(d)))
    keep.wait()
    for d in range(1, n):
        copy(mine, tab.at[core, b, x, (a + n - d) % n], aa_s.at[d - 1], aa_r.at[d - 1], at_a(d)).wait_recv()

    def piece(away, e):
        return tab.at[core, (b + n - away) % n, (x + nx - e) % nx]

    for d in range(1, nx):
        go(copy(piece(0, 0), piece(0, 0), ax_s.at[d - 1], ax_r.at[d - 1], at_x(d)))

    def pass_on(k, e):
        go(copy(piece(k, e), piece(k, e), tw_s.at[k, e], tw_r.at[k, e], twin))

    for e in range(nx):
        if e:
            copy(piece(0, e), piece(0, e), ax_s.at[e - 1], ax_r.at[e - 1], at_x(e)).wait_recv()
        for d in (2, n - 2, 1, n - 1):
            go(copy(piece(0, e), piece(0, e), bb_s.at[d, e], bb_r.at[d, e], at_b(d)))
        pass_on(0, e)

    def land(k, e):
        copy(piece(k, e), piece(k, e), bb_s.at[k, e], bb_r.at[k, e], at_b(k)).wait_recv()

    for e in range(nx):
        for k, onward in ((2, (1, 2) if e % 2 == 0 else (1,)), (n - 2, (n - 1,) if e % 2 == 0 else (n - 1, n - 2))):
            land(k, e)
            for d in onward:
                go(copy(piece(k, e), piece(k, e), bb_s.at[(k + d) % n, e], bb_r.at[(k + d) % n, e], at_b(d)))
            pass_on(k, e)
        for k in (1, n - 1):
            land(k, e)
            pass_on(k, e)
    for e in range(nx):
        for k in (3, n - 3, 4):
            land(k, e)
            pass_on(k, e)
    theirs = z * core + y * other
    for k in range(n):
        for e in range(nx):
            ref = tab.at[other, (theirs + n - k) % n, (x + nx - e) % nx]
            copy(ref, ref, tw_s.at[k, e], tw_r.at[k, e], twin).wait_recv()
    finish()


def share(nx, n, vectors, u, v):
    depth, rows = vectors.shape
    block = rows // 2 // (nx * n)
    dma = pltpu.SemaphoreType.DMA
    tab = (2, n, nx, n, block, 128)
    hbm = pl.BlockSpec(memory_space=pltpu.MemorySpace.HBM)
    pairs = []
    for shape in ((nx - 1, 4), (n - 1,), (n - 1,), (nx - 1,), (n, nx), (n, nx)):
        pairs += [dma(shape), dma(shape)]
    return pl.pallas_call(
        functools.partial(share_kernel, nx, n),
        out_shape=jax.ShapeDtypeStruct(tab, BF16),
        in_specs=[hbm] * 3,
        out_specs=pl.BlockSpec(memory_space=pl.ANY),
        scratch_shapes=[
            pltpu.VMEM((nx, 2, depth, rows // 2 // nx), BF16),
            pltpu.VMEM((nx, 2) + u.shape, BF16),
            pltpu.VMEM((n, block, 128), F32),
            pltpu.VMEM((n - 1, block, 128), F32),
            pltpu.VMEM((block, 128), BF16),
            dma((5,)),
        ] + pairs,
        compiler_params=pltpu.CompilerParams(collective_id=0, has_side_effects=True, vmem_limit_bytes=8 << 20),
    )(vectors, u, v)


def in_hbm(t):
    return pltpu.with_memory_space_constraint(t, pltpu.MemorySpace.HBM)


def body(outcome_vectors, u_factor, v_factor, outcome_index):
    table = share(4, 8, in_hbm(outcome_vectors.T), in_hbm(u_factor), in_hbm(v_factor))
    return local_part(lambda: (lax.axis_index("row"), lax.axis_index("col")))(outcome_index, table)


def solution(mesh):
    placed = (P("row", "col"), P(None, "col"), P(None, "col"), P())
    return jax.shard_map(
        body, mesh=mesh, in_specs=placed, out_specs=P("row", "col"), check_vma=False
    )
```
